512 devices in a mesh: sector: 64 (over y, z), term: 8 (over x, core).
Axes of the slice: x: 4, y: 8, z: 8, core: 2. Of those that a mesh axis runs over, the one named last changes fastest.
Arguments:
- psi: bfloat16 [4, 64, 4, 256, 256], P(None, 'sector'), may hold values from -6 to 6
- left_env: bfloat16 [16, 64, 256, 256], P('term', 'sector'), may hold values from -0.375 to 0.375
- right_env: bfloat16 [16, 64, 256, 256], P('term', 'sector'), may hold values from -0.375 to 0.375
- op_index: int32 [16], P('term'), may hold values from 0 to 4
- kept_rows: int32 [64], P('sector'), may hold values from 64 to 256, as said below
Outputs:
- sigma: float32 [4, 64, 4, 256, 256], P(None, 'sector', None, 'term')
The draws below stay inside these ranges and needn't reach their ends.
Inputs may be any that keep to these rules, and one draw needn't show every extreme that they name: `kept_rows`: some sector keeps all 256 rows and some other keeps 256 // 4.
All inputs are finite; a program needn't handle non-finite values.
Results may differ from the reference program's by a relative error of at most 0.0029.
Values may be sent and summed in bfloat16 or wider, within the bound.
A program may use at most 64 MiB of HBM per device.

```python
import jax
import jax.numpy as jnp
from jax import lax

B = 256
PHYS = 4
OP_KINDS = 5
NVEC = 4
TERMS = 16
SECTORS = 64


def draw_kept_rows(key, part):
    key_sizes, key_full, key_small = jax.random.split(jax.random.fold_in(key, 17), 3)
    counts = jax.random.randint(key_sizes, (SECTORS,), B // 4, B + 1, dtype=jnp.int32)
    full_index = jax.random.randint(key_full, (), 0, SECTORS, dtype=jnp.int32)
    small_index = (full_index + 1 + jax.random.randint(key_small, (), 0, SECTORS - 1, dtype=jnp.int32)) % SECTORS
    counts = counts.at[full_index].set(B).at[small_index].set(B // 4)
    return counts


def place_ends(drawn, stream_key, smallest, top_value):
    spot = [jax.random.randint(jax.random.fold_in(stream_key, axis), (), 0, length) for axis, length in enumerate(drawn.shape)]
    widest = drawn.shape.index(max(drawn.shape))
    neighbour = spot[:widest] + [(spot[widest] + 1) % drawn.shape[widest]] + spot[widest + 1:]
    return drawn.at[tuple(spot)].set(smallest).at[tuple(neighbour)].set(top_value)


def level_of(stream_key, shape, pieces, smallest, top_value):
    gain, own = 1.0, jax.random.fold_in(stream_key, 6)
    for position, parts in pieces:
        steps = jnp.exp(jax.random.uniform(jax.random.fold_in(own, position), (parts,), jnp.float32, smallest / len(pieces), top_value / len(pieces)))
        gain = gain * jnp.repeat(steps, shape[position] // parts).reshape([-1 if axis == position else 1 for axis in range(len(shape))])
    return gain


def normal_values(key, extent, scale, reach, shards=(), held_as=jnp.bfloat16):
    entries = jax.random.normal(key, extent, jnp.float32) * scale
    if len(shards) > 0:
        entries = level_of(key, extent, shards, -0.22, 0.18) * entries
    return jnp.clip(entries, min=-reach, max=reach).astype(held_as)


def setup_inputs(seed: int = 0) -> dict:
    keys = jax.random.split(jax.random.key(seed), 6)
    psi = normal_values(keys[0], (NVEC, SECTORS, PHYS, B, B), 1.0, 6.0, ((1, 64),))
    left_env = normal_values(keys[1], (TERMS, SECTORS, B, B), B ** -0.5, 0.375, ((0, 8), (1, 64)))
    right_env = normal_values(keys[2], (TERMS, SECTORS, B, B), B ** -0.5, 0.375, ((0, 8), (1, 64)))
    op_index = place_ends(jax.random.randint(keys[3], (TERMS,), 0, OP_KINDS), jax.random.fold_in(keys[3], 1), 0, OP_KINDS - 1).astype(jnp.int32)
    kept_rows = draw_kept_rows(jax.random.fold_in(keys[5], 71), 0)
    return {"psi": psi, "left_env": left_env, "right_env": right_env, "op_index": op_index, "kept_rows": kept_rows}


def diagonal_matrix(values):
    return [[values[r] if r == c else 0.0 for c in range(4)] for r in range(4)]


def operator_table():
    flip = [[0.0, 0.0, 0.0, 0.0], [0.0, 0.0, 0.5, 0.0], [0.0, 0.5, 0.0, 0.0], [0.0, 0.0, 0.0, 0.0]]
    stacked = [diagonal_matrix([1.0, 1.0, 1.0, 1.0]), diagonal_matrix([0.25, -0.25, -0.25, 0.25]), flip, diagonal_matrix([0.5, 0.5, -0.5, -0.5]), diagonal_matrix([0.5, -0.5, 0.5, -0.5])]
    return jnp.asarray(stacked, jnp.float32)


def reference(psi, left_env, right_env, op_index, kept_rows):
    onehot = (op_index[:, None] == jnp.arange(OP_KINDS, dtype=jnp.int32)[None, :]).astype(jnp.float32)
    term_factor = jnp.einsum("tk,kpq->tpq", onehot, operator_table(), precision=lax.Precision.HIGHEST)
    trial_vectors = psi.astype(jnp.float32)
    zeros_block = jnp.zeros((1, B, B), jnp.float32)

    def per_term(running, inputs_per_term):
        left_mat, right_mat, coeff_mat = inputs_per_term
        lifted = jnp.einsum("sab,vspbc->vspac", left_mat.astype(jnp.float32), trial_vectors, precision=lax.Precision.HIGHEST)
        lifted = lax.optimization_barrier(lifted.astype(jnp.bfloat16)).astype(jnp.float32)
        right_f = right_mat.astype(jnp.float32)
        upper_right_block = jnp.concatenate([right_f[1:], zeros_block], 0)
        right_down = jnp.concatenate([zeros_block, right_f[:-1]], 0)
        chosen = jnp.stack([upper_right_block, right_f, right_f, right_down], 1)
        mapped_vectors = jnp.einsum("vspac,spdc->vspad", lifted, chosen, precision=lax.Precision.HIGHEST)
        running = running + jnp.einsum("pq,vsqad->vspad", coeff_mat, mapped_vectors, precision=lax.Precision.HIGHEST)
        return running, None

    start = jnp.zeros((NVEC, SECTORS, PHYS, B, B), jnp.float32)
    summed, _ = lax.scan(per_term, start, (left_env, right_env, term_factor))
    zero_count = jnp.zeros((1,), jnp.int32)
    kept_up = jnp.concatenate([kept_rows[1:], zero_count], 0)
    kept_down = jnp.concatenate([zero_count, kept_rows[:-1]], 0)
    column_kept = jnp.stack([kept_up, kept_rows, kept_rows, kept_down], 1)
    row_ids = jnp.arange(B, dtype=jnp.int32)
    keep_mask = (row_ids[None, None, :, None] < kept_rows[:, None, None, None]) & (row_ids[None, None, None, :] < column_kept[:, :, None, None])
    return jnp.where(keep_mask[None], summed, 0.0)
```

```python
import functools

import jax
import jax.numpy as jnp
from jax import lax
from jax.experimental import pallas as pl
from jax.experimental.pallas import tpu as pltpu
from jax.sharding import PartitionSpec as P

F32 = jnp.float32
BF16 = jnp.bfloat16
NX = 4


def local(src, dst, sem):
    return pltpu.make_async_copy(src, dst, sem)


def remote(src, dst, send, recv, dev):
    return pltpu.make_async_remote_copy(
        src_ref=src, dst_ref=dst, send_sem=send, recv_sem=recv, device_id=dev, device_id_type=pl.DeviceIdType.MESH
    )


def nt_dot(a, b):
    return lax.dot_general(a, b, (((1,), (1,)), ((), ())), preferred_element_type=F32)


def kernel(
    sectors, psi, left, right, op, kept, out,
    pin, pout, lraw, lin, lout, rown, rnbr, mo, mall, mz,
    sb, kf, rs, ry, rx, po, loc, ob,
    s_load, s_pl, r_pl, s_pr, r_pr, s_pm, r_pm, s_zr, r_zr, s_zm, r_zm,
    s_d2, r_ry, s_dir, s_rel, r_rx, s_po, r_po, s_out,
):
    nvec, _, size, _ = psi.shape
    rc, rd = size // NX, size // NX // 2
    s = lax.axis_index("sector")
    k = lax.axis_index("term")
    x, c = lax.div(k, 2), lax.rem(k, 2)
    up = lax.rem(s + 1, sectors)
    down = lax.rem(s + sectors - 1, sectors)
    plus = lax.rem(x + 1, NX)
    minus = lax.rem(x + NX - 1, NX)
    partner = (s, 2 * x + 1 - c)
    own2 = pl.ds(2 * c, 2)
    chips = [lax.rem(x + off, NX) for off in (2, 1, 3, 0)]
    toward = [plus, minus]

    loads = [local(left.at[:, chips[i]], lraw.at[own2, pl.ds(i * rc, rc)], s_load.at[i]) for i in range(4)]
    loads += [
        local(right, rown.at[own2], s_load.at[4]),
        local(psi.at[:, 1 + c], pin.at[:, 0], s_load.at[5]),
        local(psi.at[:, 2 - c], pin.at[:, 1], s_load.at[6]),
        local(psi.at[:, 3 * c], pout, s_load.at[7]),
    ]
    for copy in loads:
        copy.start()
    row8 = lax.broadcasted_iota(jnp.int32, mo.shape, 0)
    mo[...] = jnp.where(row8 == 0, kept[0], jnp.where(row8 == 1, op[0], op[1]))
    mall[c] = mo[...]

    barrier = pltpu.get_barrier_semaphore()
    source = jnp.where(c == 0, up, down)
    greet = [partner, (source, 2 * x), (source, 2 * x + 1)]
    greet += [(s, 2 * t + h) for t in toward for h in range(2)]
    for dev in greet:
        pl.semaphore_signal(barrier, inc=1, device_id=dev, device_id_type=pl.DeviceIdType.MESH)
    pl.semaphore_wait(barrier, len(greet))

    give_left = [
        remote(left.at[:, chips[i]], lraw.at[own2, pl.ds(i * rc, rc)], s_pl.at[i], r_pl.at[i], partner)
        for i in range(4)
    ]
    give_right = remote(right, rown.at[own2], s_pr.at[0], r_pr.at[0], partner)
    give_meta = remote(mo, mall.at[c], s_pm.at[0], r_pm.at[0], partner)
    zdev = [(down, 2 * x), (up, 2 * x + 1)]
    give_z = [
        remote(right.at[t], rnbr.at[2 * c + t], s_zr.at[i, t], r_zr.at[c, t], zdev[i]) for t in range(2) for i in range(2)
    ]
    give_zm = [remote(mo, mz.at[c], s_zm.at[i], r_zm.at[c], zdev[i]) for i in range(2)]
    for copy in [give_meta, *give_left, give_right, *give_z, *give_zm]:
        copy.start()

    sign = jnp.where(c == 0, 0.5, -0.5).astype(F32)

    def scale_left(cc):
        for t in range(2):
            which = mall[cc, pl.ds(1 + t, 1), :]
            diag = jnp.where(which == 0, 1.0, jnp.where(which == 1, -0.25, 0.0))
            diag = jnp.where(which == 3, sign, jnp.where(which == 4, -sign, diag))
            flip = jnp.where(which == 2, 0.5, 0.0)
            outer = jnp.where(which == 0, 1.0, jnp.where(which == 1, 0.25, 0.0))
            outer = jnp.where(which >= 3, sign, outer)
            mat = lraw[2 * cc + t].astype(F32)
            lin[2 * cc + t, :, :size] = (mat * diag).astype(BF16)
            lin[2 * cc + t, :, size:] = (mat * flip).astype(BF16)
            lout[2 * cc + t] = (mat * outer).astype(BF16)

    for copy in loads[:5]:
        copy.wait()
    scale_left(c)
    give_meta.wait_recv()
    for copy in give_left:
        copy.wait_recv()
    scale_left(1 - c)
    give_right.wait_recv()
    for copy in loads[5:]:
        copy.wait()

    column = lax.broadcasted_iota(jnp.int32, (size, size), 1)

    def give_far(g, v, sgn):
        return remote(sb.at[g, v, 0], ry.at[g, v], s_d2.at[g, v], r_ry.at[g, v], (s, 2 * toward[sgn] + c))

    def give_near(g, v, sgn, h):
        return remote(
            sb.at[g, v, 1, pl.ds(h * rd, rd)], rx.at[1 - sgn, c, g, v], s_dir.at[g, v, h], r_rx.at[1 - sgn, c, g, v],
            (s, 2 * toward[1 - sgn] + h),
        )

    def give_relay(g, v, sgn, h):
        return remote(
            rs.at[g, v, pl.ds(h * rd, rd)], rx.at[sgn, c, g, v], s_rel.at[g, v, h], r_rx.at[sgn, c, g, v],
            (s, 2 * toward[sgn] + h),
        )

    def give_chip(g, v):
        return remote(po.at[g, v], loc.at[c, g, v], s_po.at[g, v], r_po.at[g, v], partner)

    def compute(g, limit):
        lmat, pmat, rmat = (lin, pin, rown) if g == 0 else (lout, pout, rnbr)

        def step(jj, carry):
            for sgn in range(2):
                v = jj + 2 * sgn
                vec = pmat[v].reshape(-1, size)
                total = jnp.zeros((size, size), F32)
                for t in range(4):
                    lifted = jnp.dot(lmat[t], vec, preferred_element_type=F32).astype(BF16)
                    total += nt_dot(lifted, rmat[t])
                total = jnp.where(column < limit, total, 0.0)
                parts = [total[i * rc : (i + 1) * rc] for i in range(4)]
                sb[g, v, 0] = parts[0].astype(BF16)
                sb[g, v, 1] = parts[2 - sgn].astype(BF16)
                give_far(g, v, sgn).start()
                for h in range(2):
                    give_near(g, v, sgn, h).start()
                kf[g, v] = parts[1 + sgn]
                first, second = parts[3][:rd], parts[3][rd:]
                loc[c, g, v] = jnp.where(c == 0, first, second)
                po[g, v] = jnp.where(c == 0, second, first)
                give_chip(g, v).start()
            return carry

        lax.fori_loop(0, nvec // 2, step, 0)

    def relay(g):
        def step(jj, carry):
            for sgn in range(2):
                v = jj + 2 * sgn
                give_far(g, v, sgn).wait_recv()
                rs[g, v] = (kf[g, v] + ry[g, v].astype(F32)).astype(BF16)
                for h in range(2):
                    give_relay(g, v, sgn, h).start()
            return carry

        lax.fori_loop(0, nvec // 2, step, 0)

    row = lax.broadcasted_iota(jnp.int32, (rd, size), 0) + k * rd
    mine = mo[pl.ds(0, 1), :]

    def give_out(v, p):
        return local(ob.at[v, p], out.at[v, p], s_out.at[v, p])

    def arrival(side, cc, g, v):
        return remote(rx.at[side, cc, g, v], rx.at[side, cc, g, v], s_po.at[g, v], r_rx.at[side, cc, g, v], partner)

    def finish(g):
        def step(v, carry):
            give_chip(g, v).wait_recv()
            for cc in range(2):
                p = 3 * cc if g else 1 + cc
                for side in range(2):
                    arrival(side, cc, g, v).wait_recv()
                total = loc[cc, g, v] + rx[0, cc, g, v].astype(F32) + rx[1, cc, g, v].astype(F32)
                ob[v, p] = jnp.where(row < mine, total, 0.0)
                give_out(v, p).start()
            return carry

        lax.fori_loop(0, nvec, step, 0)

    compute(0, mine)
    relay(0)
    for cc in range(2):
        for t in range(2):
            remote(right.at[t], rnbr.at[2 * cc + t], s_zr.at[0, t], r_zr.at[cc, t], partner).wait_recv()
        remote(mo, mz.at[cc], s_zm.at[0], r_zm.at[cc], partner).wait_recv()
    edge = jnp.where(c == 0, sectors - 1, 0)
    compute(1, jnp.where(s == edge, 0, mz[0, pl.ds(0, 1), :]))
    finish(0)
    relay(1)
    finish(1)

    for copy in [give_meta, *give_left, give_right, *give_z, *give_zm]:
        copy.wait_send()

    def drain(v, carry):
        for g in range(2):
            give_far(g, v, 0).wait_send()
            for h in range(2):
                give_near(g, v, 0, h).wait_send()
                give_relay(g, v, 0, h).wait_send()
            give_chip(g, v).wait_send()
        for p in range(4):
            give_out(v, p).wait()
        return carry

    lax.fori_loop(0, nvec, drain, 0)


def shards(psi, left, right, op, kept):
    nvec, _, phys, size, _ = psi.shape
    rc, rd = size // NX, size // NX // 2
    sectors = lax.axis_size("sector")
    dma = pltpu.SemaphoreType.DMA
    vmem = pltpu.VMEM
    scratch = [
        vmem((nvec, 2, size, size), BF16),
        vmem((nvec, size, size), BF16),
        vmem((4, size, size), BF16),
        vmem((4, size, 2 * size), BF16),
        vmem((4, size, size), BF16),
        vmem((4, size, size), BF16),
        vmem((4, size, size), BF16),
        vmem((8, size), jnp.int32),
        vmem((2, 8, size), jnp.int32),
        vmem((2, 8, size), jnp.int32),
        vmem((2, nvec, 2, rc, size), BF16),
        vmem((2, nvec, rc, size), F32),
        vmem((2, nvec, rc, size), BF16),
        vmem((2, nvec, rc, size), BF16),
        vmem((2, 2, 2, nvec, rd, size), BF16),
        vmem((2, nvec, rd, size), F32),
        vmem((2, 2, nvec, rd, size), F32),
        vmem((nvec, phys, rd, size), F32),
        dma((8,)),
        dma((4,)), dma((4,)), dma((1,)), dma((1,)), dma((1,)), dma((1,)),
        dma((2, 2)), dma((2, 2)), dma((2,)), dma((2,)),
        dma((2, nvec)), dma((2, nvec)), dma((2, nvec, 2)), dma((2, nvec, 2)), dma((2, 2, 2, nvec)),
        dma((2, nvec)), dma((2, nvec)), dma((nvec, phys)),
    ]
    anyspace = pl.BlockSpec(memory_space=pl.ANY)
    smem = pl.BlockSpec(memory_space=pltpu.SMEM)
    result = pl.pallas_call(
        functools.partial(kernel, sectors),
        out_shape=jax.ShapeDtypeStruct((nvec, phys, rd, size), F32),
        in_specs=[anyspace, anyspace, anyspace, smem, smem],
        out_specs=anyspace,
        scratch_shapes=scratch,
        compiler_params=pltpu.CompilerParams(collective_id=0, has_side_effects=True),
    )(
        psi.reshape(nvec, phys, size, size),
        left.reshape(2, NX, rc, size),
        right.reshape(2, size, size),
        op,
        kept,
    )
    return result[:, None]


def solution(mesh):
    in_specs = (
        P(None, "sector", None, None, None),
        P("term", "sector", None, None),
        P("term", "sector", None, None),
        P("term"),
        P("sector"),
    )
    out_specs = P(None, "sector", None, "term", None)
    return jax.shard_map(shards, mesh=mesh, in_specs=in_specs, out_specs=out_specs, check_vma=False)
```

```python
import functools

import jax
import jax.numpy as jnp
from jax import lax
from jax.experimental import pallas as pl
from jax.experimental.pallas import tpu as pltpu
from jax.sharding import PartitionSpec as P

F32 = jnp.float32
BF16 = jnp.bfloat16
NX = 4


def local(src, dst, sem):
    return pltpu.make_async_copy(src, dst, sem)


def remote(src, dst, send, recv, dev):
    return pltpu.make_async_remote_copy(
        src_ref=src, dst_ref=dst, send_sem=send, recv_sem=recv, device_id=dev, device_id_type=pl.DeviceIdType.MESH
    )


def nt_dot(a, b):
    return lax.dot_general(a, b, (((1,), (1,)), ((), ())), preferred_element_type=F32)


def kernel(
    sectors, psi, left, right, op, kept, out,
    pin, pout, lraw, lin, lout, rown, rnbr, lf, mo, mall, mz,
    fb0, nb0, kf0, rs0, ry0, rx0, po0, loc0, fb1, nb1, kf1, rs1, ry1, rx1, po1, loc1, ob,
    s_load, s_pl, r_pl, s_pr, r_pr, s_pm, r_pm, s_zr, r_zr, s_zm, r_zm,
    s_d2, r_ry, s_dir, s_rel, r_rx, s_po, r_po, s_out,
):
    nvec, _, size, _ = psi.shape
    rc, rd = size // NX, size // NX // 2
    s = lax.axis_index("sector")
    k = lax.axis_index("term")
    x, c = lax.div(k, 2), lax.rem(k, 2)
    up = lax.rem(s + 1, sectors)
    down = lax.rem(s + sectors - 1, sectors)
    plus = lax.rem(x + 1, NX)
    minus = lax.rem(x + NX - 1, NX)
    partner = (s, 2 * x + 1 - c)
    own2 = pl.ds(2 * c, 2)
    chips = [lax.rem(x + off, NX) for off in (2, 1, 3, 0)]
    toward = [plus, minus]

    loads = [local(left.at[:, chips[i]], lraw.at[own2, pl.ds(i * rc, rc)], s_load.at[i]) for i in range(4)]
    loads += [
        local(right, rown.at[own2], s_load.at[4]),
        local(psi.at[:, 1 + c], pin.at[:, 0], s_load.at[5]),
        local(psi.at[:, 2 - c], pin.at[:, 1], s_load.at[6]),
        local(psi.at[:, 3 * c], pout, s_load.at[7]),
    ]
    for copy in loads:
        copy.start()
    row8 = lax.broadcasted_iota(jnp.int32, mo.shape, 0)
    mo[...] = jnp.where(row8 == 0, kept[0], jnp.where(row8 == 1, op[0], op[1]))
    mall[c] = mo[...]

    barrier = pltpu.get_barrier_semaphore()
    source = jnp.where(c == 0, up, down)
    greet = [partner, (source, 2 * x), (source, 2 * x + 1)]
    greet += [(s, 2 * t + h) for t in toward for h in range(2)]
    for dev in greet:
        pl.semaphore_signal(barrier, inc=1, device_id=dev, device_id_type=pl.DeviceIdType.MESH)
    pl.semaphore_wait(barrier, len(greet))

    give_left = [
        remote(left.at[:, chips[i]], lraw.at[own2, pl.ds(i * rc, rc)], s_pl.at[i], r_pl.at[i], partner)
        for i in range(4)
    ]
    give_right = remote(right, rown.at[own2], s_pr.at[0], r_pr.at[0], partner)
    give_meta = remote(mo, mall.at[c], s_pm.at[0], r_pm.at[0], partner)
    zdev = [(down, 2 * x), (up, 2 * x + 1)]
    half = size // 2
    give_z = [
        remote(
            right.at[:, pl.ds(h * half, half)], rnbr.at[own2, pl.ds(h * half, half)], s_zr.at[i, h], r_zr.at[c, h], zdev[i]
        )
        for h in range(2) for i in range(2)
    ]
    give_zm = [remote(mo, mz.at[c], s_zm.at[i], r_zm.at[c], zdev[i]) for i in range(2)]
    for copy in [give_meta, *give_left, give_right, *give_zm, *give_z]:
        copy.start()

    sign = jnp.where(c == 0, 0.5, -0.5).astype(F32)

    def scale_left(cc):
        for t in range(2):
            which = mall[cc, pl.ds(1 + t, 1), :]
            diag = jnp.where(which == 0, 1.0, jnp.where(which == 1, -0.25, 0.0))
            diag = jnp.where(which == 3, sign, jnp.where(which == 4, -sign, diag))
            flip = jnp.where(which == 2, 0.5, 0.0)
            outer = jnp.where(which == 0, 1.0, jnp.where(which == 1, 0.25, 0.0))
            outer = jnp.where(which >= 3, sign, outer)
            mat = lraw[2 * cc + t].astype(F32)
            lin[2 * cc + t, :, :size] = (mat * diag).astype(BF16)
            lin[2 * cc + t, :, size:] = (mat * flip).astype(BF16)
            lout[2 * cc + t] = (mat * outer).astype(BF16)

    for copy in loads[:5]:
        copy.wait()
    scale_left(c)
    give_meta.wait_recv()
    for copy in give_left:
        copy.wait_recv()
    scale_left(1 - c)
    give_right.wait_recv()
    for copy in loads[5:]:
        copy.wait()

    fb, nb, kf, rs, ry = (fb0, fb1), (nb0, nb1), (kf0, kf1), (rs0, rs1), (ry0, ry1)
    rx, po, loc = (rx0, rx1), (po0, po1), (loc0, loc1)

    def give_far(g, a, sgn):
        return remote(fb[g].at[a, sgn], ry[g].at[a, sgn], s_d2.at[g, a, sgn], r_ry.at[g, a, sgn], (s, 2 * toward[sgn] + c))

    def give_near(g, a, sgn, h):
        return remote(
            nb[g].at[a, sgn, h], rx[g].at[1 - sgn, c, a, sgn], s_dir.at[g, a, sgn, h], r_rx.at[g, 1 - sgn, c, a, sgn],
            (s, 2 * toward[1 - sgn] + h),
        )

    def give_relay(g, a, sgn, h):
        return remote(
            rs[g].at[a, sgn, h], rx[g].at[sgn, c, a, sgn], s_rel.at[g, a, sgn, h], r_rx.at[g, sgn, c, a, sgn],
            (s, 2 * toward[sgn] + h),
        )

    def give_chip(g, a, sgn):
        return remote(po[g].at[a, sgn], loc[g].at[c, a, sgn], s_po.at[g, a, sgn], r_po.at[g, a, sgn], partner)

    def parts_of(total):
        return [total[i * rc : (i + 1) * rc].reshape(2, rd, -1) for i in range(4)]

    def inner(jj, carry):
        for sgn in range(2):
            v = jj + 2 * sgn
            vec = pin[v].reshape(-1, size)
            total = jnp.zeros((size, size), F32)
            for t in range(4):
                lifted = jnp.dot(lin[t], vec, preferred_element_type=F32).astype(BF16)
                total += nt_dot(lifted, rown[t])
            column = lax.broadcasted_iota(jnp.int32, total.shape, 1)
            parts = parts_of(jnp.where(column < mine, total, 0.0))
            fb0[jj, sgn] = parts[0].astype(BF16)
            give_far(0, jj, sgn).start()
            nb0[jj, sgn] = parts[2 - sgn].astype(BF16)
            for h in range(2):
                give_near(0, jj, sgn, h).start()
            kf0[jj, sgn] = parts[1 + sgn]
            loc0[c, jj, sgn] = jnp.where(c == 0, parts[3][0], parts[3][1])
            po0[jj, sgn] = jnp.where(c == 0, parts[3][1], parts[3][0])
            give_chip(0, jj, sgn).start()
        return carry

    def lift_outer(v, carry):
        for t in range(4):
            lf[v, t] = jnp.dot(lout[t], pout[v], preferred_element_type=F32).astype(BF16)
        return carry

    def outer(a, limit):
        for sgn in range(2):
            for jj in range(2):
                total = jnp.zeros((size, half), F32)
                for t in range(4):
                    total += nt_dot(lf[2 * sgn + jj, t], rnbr[t, pl.ds(a * half, half), :])
                column = lax.broadcasted_iota(jnp.int32, total.shape, 1) + a * half
                parts = parts_of(jnp.where(column < limit, total, 0.0))
                fb1[a, sgn, :, jj] = parts[0].astype(BF16)
                nb1[a, sgn, :, jj] = parts[2 - sgn].astype(BF16)
                kf1[a, sgn, :, jj] = parts[1 + sgn]
                loc1[c, a, sgn, jj] = jnp.where(c == 0, parts[3][0], parts[3][1])
                po1[a, sgn, jj] = jnp.where(c == 0, parts[3][1], parts[3][0])
            give_far(1, a, sgn).start()
        for sgn in range(2):
            for h in range(2):
                give_near(1, a, sgn, h).start()
            give_chip(1, a, sgn).start()

    def relay(g, a):
        for sgn in range(2):
            give_far(g, a, sgn).wait_recv()
            rs[g][a, sgn] = (kf[g][a, sgn] + ry[g][a, sgn].astype(F32)).astype(BF16)
            for h in range(2):
                give_relay(g, a, sgn, h).start()

    row = lax.broadcasted_iota(jnp.int32, (rd, size), 0) + k * rd
    mine = mo[pl.ds(0, 1), :]

    def give_out(v, p):
        return local(ob.at[v, p], out.at[v, p], s_out.at[v, p])

    def arrival(g, side, cc, a, sgn):
        piece = rx[g].at[side, cc, a, sgn]
        return remote(piece, piece, s_po.at[g, a, sgn], r_rx.at[g, side, cc, a, sgn], partner)

    def gathered(g, cc, a, sgn):
        for side in range(2):
            arrival(g, side, cc, a, sgn).wait_recv()
        total = loc[g][cc, a, sgn]
        for side in range(2):
            total += rx[g][side, cc, a, sgn].astype(F32)
        return total

    def finish_inner(jj, carry):
        for sgn in range(2):
            v = jj + 2 * sgn
            give_chip(0, jj, sgn).wait_recv()
            for cc in range(2):
                ob[v, 1 + cc] = jnp.where(row < mine, gathered(0, cc, jj, sgn), 0.0)
                give_out(v, 1 + cc).start()
        return carry

    def finish_outer(a):
        for sgn in range(2):
            give_chip(1, a, sgn).wait_recv()
            for cc in range(2):
                total = gathered(1, cc, a, sgn)
                for jj in range(2):
                    v = 2 * sgn + jj
                    ob[v, 3 * cc, :, pl.ds(a * half, half)] = jnp.where(row[:, :half] < mine[:, :half], total[jj], 0.0)
                    if a == 1:
                        give_out(v, 3 * cc).start()

    def wait_z(h):
        for cc in range(2):
            remote(
                right.at[:, pl.ds(h * half, half)], rnbr.at[pl.ds(2 * cc, 2), pl.ds(h * half, half)],
                s_zr.at[0, h], r_zr.at[cc, h], partner,
            ).wait_recv()

    lax.fori_loop(0, nvec // 2, inner, 0)
    lax.fori_loop(0, nvec, lift_outer, 0)
    relay(0, 0)
    for cc in range(2):
        remote(mo, mz.at[cc], s_zm.at[0], r_zm.at[cc], partner).wait_recv()
    edge = jnp.where(c == 0, sectors - 1, 0)
    limit = jnp.where(s == edge, 0, mz[0, pl.ds(0, 1), :])[:, :half]
    wait_z(0)
    outer(0, limit)
    relay(0, 1)
    wait_z(1)
    outer(1, limit)
    relay(1, 0)
    lax.fori_loop(0, nvec // 2, finish_inner, 0)
    relay(1, 1)
    finish_outer(0)
    finish_outer(1)

    for copy in [give_meta, *give_left, give_right, *give_z, *give_zm]:
        copy.wait_send()

    def drain(a, carry):
        for sgn in range(2):
            for g in range(2):
                give_far(g, a, sgn).wait_send()
                for h in range(2):
                    give_near(g, a, sgn, h).wait_send()
                    give_relay(g, a, sgn, h).wait_send()
                give_chip(g, a, sgn).wait_send()
            for p in range(4):
                give_out(a + 2 * sgn, p).wait()
        return carry

    lax.fori_loop(0, nvec // 2, drain, 0)


def shards(psi, left, right, op, kept):
    nvec, _, phys, size, _ = psi.shape
    rc, rd = size // NX, size // NX // 2
    sectors = lax.axis_size("sector")
    dma = pltpu.SemaphoreType.DMA
    vmem = pltpu.VMEM
    scratch = [
        vmem((nvec, 2, size, size), BF16),
        vmem((nvec, size, size), BF16),
        vmem((4, size, size), BF16),
        vmem((4, size, 2 * size), BF16),
        vmem((4, size, size), BF16),
        vmem((4, size, size), BF16),
        vmem((4, size, size), BF16),
        vmem((nvec, 4, size, size), BF16),
        vmem((8, size), jnp.int32),
        vmem((2, 8, size), jnp.int32),
        vmem((2, 8, size), jnp.int32),
    ]
    for piece in ((rd, size), (2, rd, size // 2)):
        scratch += [
            vmem((2, 2, 2, *piece), BF16),
            vmem((2, 2, 2, *piece), BF16),
            vmem((2, 2, 2, *piece), F32),
            vmem((2, 2, 2, *piece), BF16),
            vmem((2, 2, 2, *piece), BF16),
            vmem((2, 2, 2, 2, *piece), BF16),
            vmem((2, 2, *piece), F32),
            vmem((2, 2, 2, *piece), F32),
        ]
    scratch += [
        vmem((nvec, phys, rd, size), F32),
        dma((8,)),
        dma((4,)), dma((4,)), dma((1,)), dma((1,)), dma((1,)), dma((1,)),
        dma((2, 2)), dma((2, 2)), dma((2,)), dma((2,)),
        dma((2, 2, 2)), dma((2, 2, 2)), dma((2, 2, 2, 2)), dma((2, 2, 2, 2)), dma((2, 2, 2, 2, 2)),
        dma((2, 2, 2)), dma((2, 2, 2)), dma((nvec, phys)),
    ]
    anyspace = pl.BlockSpec(memory_space=pl.ANY)
    smem = pl.BlockSpec(memory_space=pltpu.SMEM)
    result = pl.pallas_call(
        functools.partial(kernel, sectors),
        out_shape=pltpu.VMEM((nvec, phys, rd, size), F32),
        in_specs=[anyspace, anyspace, anyspace, smem, smem],
        out_specs=anyspace,
        scratch_shapes=scratch,
        compiler_params=pltpu.CompilerParams(collective_id=0, has_side_effects=True, vmem_limit_bytes=56 * 2**20),
    )(
        psi.reshape(nvec, phys, size, size),
        left.reshape(2, NX, rc, size),
        right.reshape(2, size, size),
        op,
        kept,
    )
    return result[:, None]


def solution(mesh):
    in_specs = (
        P(None, "sector", None, None, None),
        P("term", "sector", None, None),
        P("term", "sector", None, None),
        P("term"),
        P("sector"),
    )
    out_specs = P(None, "sector", None, "term", None)
    return jax.shard_map(shards, mesh=mesh, in_specs=in_specs, out_specs=out_specs, check_vma=False)
```

```python
import functools

import jax
import jax.numpy as jnp
from jax import lax
from jax.experimental import pallas as pl
from jax.experimental.pallas import tpu as pltpu
from jax.sharding import PartitionSpec as P

F32 = jnp.float32
BF16 = jnp.bfloat16
NX = 4


def local(src, dst, sem):
    return pltpu.make_async_copy(src, dst, sem)


def remote(src, dst, send, recv, dev):
    return pltpu.make_async_remote_copy(
        src_ref=src, dst_ref=dst, send_sem=send, recv_sem=recv, device_id=dev, device_id_type=pl.DeviceIdType.MESH
    )


def nt_dot(a, b):
    return lax.dot_general(a, b, (((1,), (1,)), ((), ())), preferred_element_type=F32)


def kernel(
    sectors, psi, left, right, op, kept, out,
    pin, pout, lraw, lin, lout, rown, rnbr, lf, mo, mall, mz,
    fb0, nb0, kf0, rs0, ry0, rx0, po0, loc0, fb1, nb1, kf1, rs1, ry1, rx1, po1, loc1,
    s_load, s_pl, r_pl, s_pr, r_pr, s_pm, r_pm, s_zr, r_zr, s_zm, r_zm,
    s_d2, r_ry, s_dir, s_rel, r_rx, s_po, r_po,
):
    nvec, _, size, _ = psi.shape
    rc, rd = size // NX, size // NX // 2
    s = lax.axis_index("sector")
    k = lax.axis_index("term")
    x, c = lax.div(k, 2), lax.rem(k, 2)
    up = lax.rem(s + 1, sectors)
    down = lax.rem(s + sectors - 1, sectors)
    plus = lax.rem(x + 1, NX)
    minus = lax.rem(x + NX - 1, NX)
    partner = (s, 2 * x + 1 - c)
    own2 = pl.ds(2 * c, 2)
    chips = [lax.rem(x + off, NX) for off in (2, 1, 3, 0)]
    toward = [plus, minus]

    loads = [local(left.at[:, chips[i]], lraw.at[own2, pl.ds(i * rc, rc)], s_load.at[i]) for i in range(4)]
    loads += [
        local(right, rown.at[own2], s_load.at[4]),
        local(psi.at[:, 1 + c], pin.at[:, 0], s_load.at[5]),
        local(psi.at[:, 2 - c], pin.at[:, 1], s_load.at[6]),
        local(psi.at[:, 3 * c], pout, s_load.at[7]),
    ]
    for copy in loads:
        copy.start()
    row8 = lax.broadcasted_iota(jnp.int32, mo.shape, 0)
    mo[...] = jnp.where(row8 == 0, kept[0], jnp.where(row8 == 1, op[0], op[1]))
    mall[c] = mo[...]

    barrier = pltpu.get_barrier_semaphore()
    source = jnp.where(c == 0, up, down)
    greet = [partner, (source, 2 * x), (source, 2 * x + 1)]
    greet += [(s, 2 * t + h) for t in toward for h in range(2)]
    for dev in greet:
        pl.semaphore_signal(barrier, inc=1, device_id=dev, device_id_type=pl.DeviceIdType.MESH)
    pl.semaphore_wait(barrier, len(greet))

    give_left = [
        remote(left.at[:, chips[i]], lraw.at[own2, pl.ds(i * rc, rc)], s_pl.at[i], r_pl.at[i], partner)
        for i in range(4)
    ]
    give_right = remote(right, rown.at[own2], s_pr.at[0], r_pr.at[0], partner)
    give_meta = remote(mo, mall.at[c], s_pm.at[0], r_pm.at[0], partner)
    zdev = [(down, 2 * x), (up, 2 * x + 1)]
    half = size // 2
    give_z = [
        remote(
            right.at[:, pl.ds(h * half, half)], rnbr.at[own2, pl.ds(h * half, half)], s_zr.at[i, h], r_zr.at[c, h], zdev[i]
        )
        for h in range(2) for i in range(2)
    ]
    give_zm = [remote(mo, mz.at[c], s_zm.at[i], r_zm.at[c], zdev[i]) for i in range(2)]
    for copy in [give_meta, *give_left, give_right, *give_zm, *give_z]:
        copy.start()

    sign = jnp.where(c == 0, 0.5, -0.5).astype(F32)

    def scale_left(cc):
        for t in range(2):
            which = mall[cc, pl.ds(1 + t, 1), :]
            diag = jnp.where(which == 0, 1.0, jnp.where(which == 1, -0.25, 0.0))
            diag = jnp.where(which == 3, sign, jnp.where(which == 4, -sign, diag))
            flip = jnp.where(which == 2, 0.5, 0.0)
            outer = jnp.where(which == 0, 1.0, jnp.where(which == 1, 0.25, 0.0))
            outer = jnp.where(which >= 3, sign, outer)
            mat = lraw[2 * cc + t].astype(F32)
            lin[2 * cc + t, :, :size] = (mat * diag).astype(BF16)
            lin[2 * cc + t, :, size:] = (mat * flip).astype(BF16)
            lout[2 * cc + t] = (mat * outer).astype(BF16)

    for copy in loads[:5]:
        copy.wait()
    scale_left(c)
    give_meta.wait_recv()
    for copy in give_left:
        copy.wait_recv()
    scale_left(1 - c)
    give_right.wait_recv()
    for copy in loads[5:]:
        copy.wait()

    fb, nb, kf, rs, ry = (fb0, fb1), (nb0, nb1), (kf0, kf1), (rs0, rs1), (ry0, ry1)
    rx, po, loc = (rx0, rx1), (po0, po1), (loc0, loc1)

    def give_far(g, a, sgn):
        return remote(fb[g].at[a, sgn], ry[g].at[a, sgn], s_d2.at[g, a, sgn], r_ry.at[g, a, sgn], (s, 2 * toward[sgn] + c))

    def give_near(g, a, sgn, h):
        return remote(
            nb[g].at[a, sgn, h], rx[g].at[1 - sgn, c, a, sgn], s_dir.at[g, a, sgn, h], r_rx.at[g, 1 - sgn, c, a, sgn],
            (s, 2 * toward[1 - sgn] + h),
        )

    def give_relay(g, a, sgn, h):
        return remote(
            rs[g].at[a, sgn, h], rx[g].at[sgn, c, a, sgn], s_rel.at[g, a, sgn, h], r_rx.at[g, sgn, c, a, sgn],
            (s, 2 * toward[sgn] + h),
        )

    def give_chip(g, a, sgn):
        return remote(po[g].at[a, sgn], loc[g].at[c, a, sgn], s_po.at[g, a, sgn], r_po.at[g, a, sgn], partner)

    def parts_of(total):
        return [total[i * rc : (i + 1) * rc].reshape(2, rd, -1) for i in range(4)]

    def inner(jj, carry):
        for sgn in range(2):
            v = jj + 2 * sgn
            vec = pin[v].reshape(-1, size)
            total = jnp.zeros((size, size), F32)
            for t in range(4):
                lifted = jnp.dot(lin[t], vec, preferred_element_type=F32).astype(BF16)
                total += nt_dot(lifted, rown[t])
            column = lax.broadcasted_iota(jnp.int32, total.shape, 1)
            parts = parts_of(jnp.where(column < mine, total, 0.0))
            fb0[jj, sgn] = parts[0].astype(BF16)
            give_far(0, jj, sgn).start()
            nb0[jj, sgn] = parts[2 - sgn].astype(BF16)
            for h in range(2):
                give_near(0, jj, sgn, h).start()
            kf0[jj, sgn] = parts[1 + sgn]
            loc0[c, jj, sgn] = jnp.where(c == 0, parts[3][0], parts[3][1])
            po0[jj, sgn] = jnp.where(c == 0, parts[3][1], parts[3][0])
            give_chip(0, jj, sgn).start()
        return carry

    def lift_outer(v, carry):
        for t in range(4):
            lf[v, t] = jnp.dot(lout[t], pout[v], preferred_element_type=F32).astype(BF16)
        return carry

    def outer(a, limit):
        for sgn in range(2):
            for jj in range(2):
                total = jnp.zeros((size, half), F32)
                for t in range(4):
                    total += nt_dot(lf[2 * sgn + jj, t], rnbr[t, pl.ds(a * half, half), :])
                column = lax.broadcasted_iota(jnp.int32, total.shape, 1) + a * half
                parts = parts_of(jnp.where(column < limit, total, 0.0))
                fb1[a, sgn, :, jj] = parts[0].astype(BF16)
                nb1[a, sgn, :, jj] = parts[2 - sgn].astype(BF16)
                kf1[a, sgn, :, jj] = parts[1 + sgn]
                loc1[c, a, sgn, jj] = jnp.where(c == 0, parts[3][0], parts[3][1])
                po1[a, sgn, jj] = jnp.where(c == 0, parts[3][1], parts[3][0])
            give_far(1, a, sgn).start()
        for sgn in range(2):
            for h in range(2):
                give_near(1, a, sgn, h).start()
            give_chip(1, a, sgn).start()

    def relay(g, a):
        for sgn in range(2):
            give_far(g, a, sgn).wait_recv()
            rs[g][a, sgn] = (kf[g][a, sgn] + ry[g][a, sgn].astype(F32)).astype(BF16)
            for h in range(2):
                give_relay(g, a, sgn, h).start()

    row = lax.broadcasted_iota(jnp.int32, (rd, size), 0) + k * rd
    mine = mo[pl.ds(0, 1), :]

    def arrival(g, side, cc, a, sgn):
        piece = rx[g].at[side, cc, a, sgn]
        return remote(piece, piece, s_po.at[g, a, sgn], r_rx.at[g, side, cc, a, sgn], partner)

    def gathered(g, cc, a, sgn):
        for side in range(2):
            arrival(g, side, cc, a, sgn).wait_recv()
        total = loc[g][cc, a, sgn]
        for side in range(2):
            total += rx[g][side, cc, a, sgn].astype(F32)
        return total

    def finish_inner(jj, carry):
        for sgn in range(2):
            v = jj + 2 * sgn
            give_chip(0, jj, sgn).wait_recv()
            for cc in range(2):
                out[v, 1 + cc] = jnp.where(row < mine, gathered(0, cc, jj, sgn), 0.0)
        return carry

    def finish_outer(a):
        for sgn in range(2):
            give_chip(1, a, sgn).wait_recv()
            for cc in range(2):
                total = gathered(1, cc, a, sgn)
                for jj in range(2):
                    v = 2 * sgn + jj
                    out[v, 3 * cc, :, pl.ds(a * half, half)] = jnp.where(row[:, :half] < mine[:, :half], total[jj], 0.0)

    def wait_z(h):
        for cc in range(2):
            remote(
                right.at[:, pl.ds(h * half, half)], rnbr.at[pl.ds(2 * cc, 2), pl.ds(h * half, half)],
                s_zr.at[0, h], r_zr.at[cc, h], partner,
            ).wait_recv()

    lax.fori_loop(0, nvec // 2, inner, 0)
    lax.fori_loop(0, nvec, lift_outer, 0)
    relay(0, 0)
    for cc in range(2):
        remote(mo, mz.at[cc], s_zm.at[0], r_zm.at[cc], partner).wait_recv()
    edge = jnp.where(c == 0, sectors - 1, 0)
    limit = jnp.where(s == edge, 0, mz[0, pl.ds(0, 1), :])[:, :half]
    wait_z(0)
    outer(0, limit)
    relay(0, 1)
    wait_z(1)
    outer(1, limit)
    relay(1, 0)
    lax.fori_loop(0, nvec // 2, finish_inner, 0)
    relay(1, 1)
    finish_outer(0)
    finish_outer(1)

    for copy in [give_meta, *give_left, give_right, *give_z, *give_zm]:
        copy.wait_send()

    def drain(a, carry):
        for sgn in range(2):
            for g in range(2):
                give_far(g, a, sgn).wait_send()
                for h in range(2):
                    give_near(g, a, sgn, h).wait_send()
                    give_relay(g, a, sgn, h).wait_send()
                give_chip(g, a, sgn).wait_send()
        return carry

    lax.fori_loop(0, nvec // 2, drain, 0)


def shards(psi, left, right, op, kept):
    nvec, _, phys, size, _ = psi.shape
    rc, rd = size // NX, size // NX // 2
    sectors = lax.axis_size("sector")
    dma = pltpu.SemaphoreType.DMA
    vmem = pltpu.VMEM
    scratch = [
        vmem((nvec, 2, size, size), BF16),
        vmem((nvec, size, size), BF16),
        vmem((4, size, size), BF16),
        vmem((4, size, 2 * size), BF16),
        vmem((4, size, size), BF16),
        vmem((4, size, size), BF16),
        vmem((4, size, size), BF16),
        vmem((nvec, 4, size, size), BF16),
        vmem((8, size), jnp.int32),
        vmem((2, 8, size), jnp.int32),
        vmem((2, 8, size), jnp.int32),
    ]
    for piece in ((rd, size), (2, rd, size // 2)):
        scratch += [
            vmem((2, 2, 2, *piece), BF16),
            vmem((2, 2, 2, *piece), BF16),
            vmem((2, 2, 2, *piece), F32),
            vmem((2, 2, 2, *piece), BF16),
            vmem((2, 2, 2, *piece), BF16),
            vmem((2, 2, 2, 2, *piece), BF16),
            vmem((2, 2, *piece), F32),
            vmem((2, 2, 2, *piece), F32),
        ]
    scratch += [
        dma((8,)),
        dma((4,)), dma((4,)), dma((1,)), dma((1,)), dma((1,)), dma((1,)),
        dma((2, 2)), dma((2, 2)), dma((2,)), dma((2,)),
        dma((2, 2, 2)), dma((2, 2, 2)), dma((2, 2, 2, 2)), dma((2, 2, 2, 2)), dma((2, 2, 2, 2, 2)),
        dma((2, 2, 2)), dma((2, 2, 2)),
    ]
    anyspace = pl.BlockSpec(memory_space=pl.ANY)
    smem = pl.BlockSpec(memory_space=pltpu.SMEM)
    result = pl.pallas_call(
        functools.partial(kernel, sectors),
        out_shape=pltpu.VMEM((nvec, phys, rd, size), F32),
        in_specs=[anyspace, anyspace, anyspace, smem, smem],
        out_specs=pl.BlockSpec(memory_space=pltpu.VMEM),
        scratch_shapes=scratch,
        compiler_params=pltpu.CompilerParams(collective_id=0, has_side_effects=True, vmem_limit_bytes=56 * 2**20),
    )(
        psi.reshape(nvec, phys, size, size),
        left.reshape(2, NX, rc, size),
        right.reshape(2, size, size),
        op,
        kept,
    )
    return result[:, None]


def solution(mesh):
    in_specs = (
        P(None, "sector", None, None, None),
        P("term", "sector", None, None),
        P("term", "sector", None, None),
        P("term"),
        P("sector"),
    )
    out_specs = P(None, "sector", None, "term", None)
    return jax.shard_map(shards, mesh=mesh, in_specs=in_specs, out_specs=out_specs, check_vma=False)
```

```python
import functools

import jax
import jax.numpy as jnp
from jax import lax
from jax.experimental import pallas as pl
from jax.experimental.pallas import tpu as pltpu
from jax.sharding import PartitionSpec as P

F32 = jnp.float32
BF16 = jnp.bfloat16
NX = 4


def local(src, dst, sem):
    return pltpu.make_async_copy(src, dst, sem)


def remote(src, dst, send, recv, dev):
    return pltpu.make_async_remote_copy(
        src_ref=src, dst_ref=dst, send_sem=send, recv_sem=recv, device_id=dev, device_id_type=pl.DeviceIdType.MESH
    )


def nt_dot(a, b):
    return lax.dot_general(a, b, (((1,), (1,)), ((), ())), preferred_element_type=F32)


def kernel(
    sectors, psi, left, right, op, kept, out,
    pin, pout, lraw, lin, lout, rown, rnbr, lf, mo, mall, mz,
    fb0, nb0, kf0, rs0, ry0, rx0, po0, loc0, fb1, nb1, kf1, rs1, ry1, rx1, po1, loc1,
    s_load, s_pl, r_pl, s_pr, r_pr, s_pm, r_pm, s_zr, r_zr, s_zm, r_zm,
    s_d2, r_ry, s_dir, s_rel, r_rx, s_po, r_po,
):
    nvec, _, size, _ = psi.shape
    rc, rd = size // NX, size // NX // 2
    s = lax.axis_index("sector")
    k = lax.axis_index("term")
    x, c = lax.div(k, 2), lax.rem(k, 2)
    up = lax.rem(s + 1, sectors)
    down = lax.rem(s + sectors - 1, sectors)
    plus = lax.rem(x + 1, NX)
    minus = lax.rem(x + NX - 1, NX)
    partner = (s, 2 * x + 1 - c)
    own2 = pl.ds(2 * c, 2)
    chips = [lax.rem(x + off, NX) for off in (2, 1, 3, 0)]
    toward = [plus, minus]

    loads = [local(left.at[:, chips[i]], lraw.at[own2, pl.ds(i * rc, rc)], s_load.at[i]) for i in range(4)]
    loads += [
        local(right, rown.at[own2], s_load.at[4]),
        local(psi.at[:, 1 + c], pin.at[:, 0], s_load.at[5]),
        local(psi.at[:, 2 - c], pin.at[:, 1], s_load.at[6]),
        local(psi.at[:, 3 * c], pout, s_load.at[7]),
    ]
    for copy in loads:
        copy.start()
    row8 = lax.broadcasted_iota(jnp.int32, mo.shape, 0)
    mo[...] = jnp.where(row8 == 0, kept[0], jnp.where(row8 == 1, op[0], op[1]))
    mall[c] = mo[...]

    barrier = pltpu.get_barrier_semaphore()
    source = jnp.where(c == 0, up, down)
    greet = [partner, (source, 2 * x), (source, 2 * x + 1)]
    greet += [(s, 2 * t + h) for t in toward for h in range(2)]
    for dev in greet:
        pl.semaphore_signal(barrier, inc=1, device_id=dev, device_id_type=pl.DeviceIdType.MESH)
    pl.semaphore_wait(barrier, len(greet))

    give_left = [
        remote(left.at[:, chips[i]], lraw.at[own2, pl.ds(i * rc, rc)], s_pl.at[i], r_pl.at[i], partner)
        for i in range(4)
    ]
    give_right = remote(right, rown.at[own2], s_pr.at[0], r_pr.at[0], partner)
    give_meta = remote(mo, mall.at[c], s_pm.at[0], r_pm.at[0], partner)
    zdev = [(down, 2 * x), (up, 2 * x + 1)]
    half = size // 2
    give_z = [
        remote(
            right.at[:, pl.ds(h * half, half)], rnbr.at[own2, pl.ds(h * half, half)], s_zr.at[i, h], r_zr.at[c, h], zdev[i]
        )
        for h in range(2) for i in range(2)
    ]
    give_zm = [remote(mo, mz.at[c], s_zm.at[i], r_zm.at[c], zdev[i]) for i in range(2)]
    for copy in [give_meta, *give_left, give_right, *give_zm, *give_z]:
        copy.start()

    sign = jnp.where(c == 0, 0.5, -0.5).astype(F32)

    def scale_left(cc):
        for t in range(2):
            which = mall[cc, pl.ds(1 + t, 1), :]
            diag = jnp.where(which == 0, 1.0, jnp.where(which == 1, -0.25, 0.0))
            diag = jnp.where(which == 3, sign, jnp.where(which == 4, -sign, diag))
            flip = jnp.where(which == 2, 0.5, 0.0)
            outer = jnp.where(which == 0, 1.0, jnp.where(which == 1, 0.25, 0.0))
            outer = jnp.where(which >= 3, sign, outer)
            mat = lraw[2 * cc + t].astype(F32)
            lin[2 * cc + t, :, :size] = (mat * diag).astype(BF16)
            lin[2 * cc + t, :, size:] = (mat * flip).astype(BF16)
            lout[2 * cc + t] = (mat * outer).astype(BF16)

    for copy in loads[:5]:
        copy.wait()
    scale_left(c)
    give_meta.wait_recv()
    for copy in give_left:
        copy.wait_recv()
    scale_left(1 - c)
    give_right.wait_recv()
    for copy in loads[5:]:
        copy.wait()

    fb, nb, kf, rs, ry = (fb0, fb1), (nb0, nb1), (kf0, kf1), (rs0, rs1), (ry0, ry1)
    rx, po, loc = (rx0, rx1), (po0, po1), (loc0, loc1)

    def give_far(g, a, sgn):
        return remote(fb[g].at[a, sgn], ry[g].at[a, sgn], s_d2.at[g, a, sgn], r_ry.at[g, a, sgn], (s, 2 * toward[sgn] + c))

    def give_near(g, a, sgn, h):
        return remote(
            nb[g].at[a, sgn, h], rx[g].at[1 - sgn, c, a, sgn], s_dir.at[g, a, sgn, h], r_rx.at[g, 1 - sgn, c, a, sgn],
            (s, 2 * toward[1 - sgn] + h),
        )

    def give_relay(g, a, sgn, h):
        return remote(
            rs[g].at[a, sgn, h], rx[g].at[sgn, c, a, sgn], s_rel.at[g, a, sgn, h], r_rx.at[g, sgn, c, a, sgn],
            (s, 2 * toward[sgn] + h),
        )

    def give_chip(g, a, sgn):
        return remote(po[g].at[a, sgn], loc[g].at[c, a, sgn], s_po.at[g, a, sgn], r_po.at[g, a, sgn], partner)

    def parts_of(total):
        return [total[i * rc : (i + 1) * rc].reshape(2, rd, -1) for i in range(4)]

    def inner(jj, carry):
        for sgn in range(2):
            v = jj + 2 * sgn
            vec = pin[v].reshape(-1, size)
            total = jnp.zeros((size, size), F32)
            for t in range(4):
                lifted = jnp.dot(lin[t], vec, preferred_element_type=F32).astype(BF16)
                total += nt_dot(lifted, rown[t])
            column = lax.broadcasted_iota(jnp.int32, total.shape, 1)
            parts = parts_of(jnp.where(column < mine, total, 0.0))
            fb0[jj, sgn] = parts[0].astype(BF16)
            give_far(0, jj, sgn).start()
            nb0[jj, sgn] = parts[2 - sgn].astype(BF16)
            for h in range(2):
                give_near(0, jj, sgn, h).start()
            kf0[jj, sgn] = parts[1 + sgn]
            loc0[c, jj, sgn] = jnp.where(c == 0, parts[3][0], parts[3][1])
            po0[jj, sgn] = jnp.where(c == 0, parts[3][1], parts[3][0])
            give_chip(0, jj, sgn).start()
        return carry

    def lift_outer(v, carry):
        for t in range(4):
            lf[v, t] = jnp.dot(lout[t], pout[v], preferred_element_type=F32).astype(BF16)
        return carry

    def outer(a, limit):
        for sgn in range(2):
            for jj in range(2):
                total = jnp.zeros((size, half), F32)
                for t in range(4):
                    total += nt_dot(lf[2 * sgn + jj, t], rnbr[t, pl.ds(a * half, half), :])
                column = lax.broadcasted_iota(jnp.int32, total.shape, 1) + a * half
                parts = parts_of(jnp.where(column < limit, total, 0.0))
                fb1[a, sgn, :, jj] = parts[0].astype(BF16)
                nb1[a, sgn, :, jj] = parts[2 - sgn].astype(BF16)
                kf1[a, sgn, :, jj] = parts[1 + sgn]
                loc1[c, a, sgn, jj] = jnp.where(c == 0, parts[3][0], parts[3][1])
                po1[a, sgn, jj] = jnp.where(c == 0, parts[3][1], parts[3][0])
            give_far(1, a, sgn).start()
            give_chip(1, a, sgn).start()

    def nears(a):
        for sgn in range(2):
            for h in range(2):
                give_near(1, a, sgn, h).start()

    def relay(g, a):
        for sgn in range(2):
            give_far(g, a, sgn).wait_recv()
            rs[g][a, sgn] = (kf[g][a, sgn] + ry[g][a, sgn].astype(F32)).astype(BF16)
            for h in range(2):
                give_relay(g, a, sgn, h).start()

    row = lax.broadcasted_iota(jnp.int32, (rd, size), 0) + k * rd
    mine = mo[pl.ds(0, 1), :]

    def arrival(g, side, cc, a, sgn):
        piece = rx[g].at[side, cc, a, sgn]
        return remote(piece, piece, s_po.at[g, a, sgn], r_rx.at[g, side, cc, a, sgn], partner)

    def gathered(g, cc, a, sgn):
        for side in range(2):
            arrival(g, side, cc, a, sgn).wait_recv()
        total = loc[g][cc, a, sgn]
        for side in range(2):
            total += rx[g][side, cc, a, sgn].astype(F32)
        return total

    def finish_inner(jj, carry):
        for sgn in range(2):
            v = jj + 2 * sgn
            give_chip(0, jj, sgn).wait_recv()
            for cc in range(2):
                out[v, 1 + cc] = jnp.where(row < mine, gathered(0, cc, jj, sgn), 0.0)
        return carry

    def finish_outer(a):
        for sgn in range(2):
            give_chip(1, a, sgn).wait_recv()
            for cc in range(2):
                total = gathered(1, cc, a, sgn)
                for jj in range(2):
                    v = 2 * sgn + jj
                    out[v, 3 * cc, :, pl.ds(a * half, half)] = jnp.where(row[:, :half] < mine[:, :half], total[jj], 0.0)

    def wait_z(h):
        for cc in range(2):
            remote(
                right.at[:, pl.ds(h * half, half)], rnbr.at[pl.ds(2 * cc, 2), pl.ds(h * half, half)],
                s_zr.at[0, h], r_zr.at[cc, h], partner,
            ).wait_recv()

    lax.fori_loop(0, nvec // 2, inner, 0)
    lax.fori_loop(0, nvec, lift_outer, 0)
    relay(0, 0)
    for cc in range(2):
        remote(mo, mz.at[cc], s_zm.at[0], r_zm.at[cc], partner).wait_recv()
    edge = jnp.where(c == 0, sectors - 1, 0)
    limit = jnp.where(s == edge, 0, mz[0, pl.ds(0, 1), :])[:, :half]
    wait_z(0)
    outer(0, limit)
    relay(0, 1)
    wait_z(1)
    outer(1, limit)
    relay(1, 0)
    nears(0)
    nears(1)
    lax.fori_loop(0, nvec // 2, finish_inner, 0)
    relay(1, 1)
    finish_outer(0)
    finish_outer(1)

    for copy in [give_meta, *give_left, give_right, *give_z, *give_zm]:
        copy.wait_send()

    def drain(a, carry):
        for sgn in range(2):
            for g in range(2):
                give_far(g, a, sgn).wait_send()
                for h in range(2):
                    give_near(g, a, sgn, h).wait_send()
                    give_relay(g, a, sgn, h).wait_send()
                give_chip(g, a, sgn).wait_send()
        return carry

    lax.fori_loop(0, nvec // 2, drain, 0)


def shards(psi, left, right, op, kept):
    nvec, _, phys, size, _ = psi.shape
    rc, rd = size // NX, size // NX // 2
    sectors = lax.axis_size("sector")
    dma = pltpu.SemaphoreType.DMA
    vmem = pltpu.VMEM
    scratch = [
        vmem((nvec, 2, size, size), BF16),
        vmem((nvec, size, size), BF16),
        vmem((4, size, size), BF16),
        vmem((4, size, 2 * size), BF16),
        vmem((4, size, size), BF16),
        vmem((4, size, size), BF16),
        vmem((4, size, size), BF16),
        vmem((nvec, 4, size, size), BF16),
        vmem((8, size), jnp.int32),
        vmem((2, 8, size), jnp.int32),
        vmem((2, 8, size), jnp.int32),
    ]
    for piece in ((rd, size), (2, rd, size // 2)):
        scratch += [
            vmem((2, 2, 2, *piece), BF16),
            vmem((2, 2, 2, *piece), BF16),
            vmem((2, 2, 2, *piece), F32),
            vmem((2, 2, 2, *piece), BF16),
            vmem((2, 2, 2, *piece), BF16),
            vmem((2, 2, 2, 2, *piece), BF16),
            vmem((2, 2, *piece), F32),
            vmem((2, 2, 2, *piece), F32),
        ]
    scratch += [
        dma((8,)),
        dma((4,)), dma((4,)), dma((1,)), dma((1,)), dma((1,)), dma((1,)),
        dma((2, 2)), dma((2, 2)), dma((2,)), dma((2,)),
        dma((2, 2, 2)), dma((2, 2, 2)), dma((2, 2, 2, 2)), dma((2, 2, 2, 2)), dma((2, 2, 2, 2, 2)),
        dma((2, 2, 2)), dma((2, 2, 2)),
    ]
    anyspace = pl.BlockSpec(memory_space=pl.ANY)
    smem = pl.BlockSpec(memory_space=pltpu.SMEM)
    result = pl.pallas_call(
        functools.partial(kernel, sectors),
        out_shape=pltpu.VMEM((nvec, phys, rd, size), F32),
        in_specs=[anyspace, anyspace, anyspace, smem, smem],
        out_specs=pl.BlockSpec(memory_space=pltpu.VMEM),
        scratch_shapes=scratch,
        compiler_params=pltpu.CompilerParams(collective_id=0, has_side_effects=True, vmem_limit_bytes=56 * 2**20),
    )(
        psi.reshape(nvec, phys, size, size),
        left.reshape(2, NX, rc, size),
        right.reshape(2, size, size),
        op,
        kept,
    )
    return result[:, None]


def solution(mesh):
    in_specs = (
        P(None, "sector", None, None, None),
        P("term", "sector", None, None),
        P("term", "sector", None, None),
        P("term"),
        P("sector"),
    )
    out_specs = P(None, "sector", None, "term", None)
    return jax.shard_map(shards, mesh=mesh, in_specs=in_specs, out_specs=out_specs, check_vma=False)
```

```python
import functools

import jax
import jax.numpy as jnp
from jax import lax
from jax.experimental import pallas as pl
from jax.experimental.pallas import tpu as pltpu
from jax.sharding import PartitionSpec as P

F32 = jnp.float32
BF16 = jnp.bfloat16
NX = 4


def local(src, dst, sem):
    return pltpu.make_async_copy(src, dst, sem)


def remote(src, dst, send, recv, dev):
    return pltpu.make_async_remote_copy(
        src_ref=src, dst_ref=dst, send_sem=send, recv_sem=recv, device_id=dev, device_id_type=pl.DeviceIdType.MESH
    )


def nt_dot(a, b):
    return lax.dot_general(a, b, (((1,), (1,)), ((), ())), preferred_element_type=F32)


def kernel(
    sectors, psi, left, right, op, kept, out,
    pin, pout, lraw, lin, lout, rown, rnbr, lf, mo, mall, mz,
    fb0, nb0, kf0, rs0, ry0, rx0, po0, loc0, fb1, nb1, kf1, rs1, ry1, rx1, po1, loc1,
    s_load, s_pl, r_pl, s_pr, r_pr, s_pm, r_pm, s_zr, r_zr, s_zm, r_zm,
    s_d2, r_ry, s_dir, s_rel, r_rx, s_po, r_po,
):
    nvec, _, size, _ = psi.shape
    rc, rd = size // NX, size // NX // 2
    s = lax.axis_index("sector")
    k = lax.axis_index("term")
    x, c = lax.div(k, 2), lax.rem(k, 2)
    up = lax.rem(s + 1, sectors)
    down = lax.rem(s + sectors - 1, sectors)
    plus = lax.rem(x + 1, NX)
    minus = lax.rem(x + NX - 1, NX)
    partner = (s, 2 * x + 1 - c)
    own2 = pl.ds(2 * c, 2)
    chips = [lax.rem(x + off, NX) for off in (2, 1, 3, 0)]
    toward = [plus, minus]

    loads = [local(left.at[:, chips[i]], lraw.at[own2, pl.ds(i * rc, rc)], s_load.at[i]) for i in range(4)]
    loads += [
        local(right, rown.at[own2], s_load.at[4]),
        local(psi.at[:, 1 + c], pin.at[:, 0], s_load.at[5]),
        local(psi.at[:, 2 - c], pin.at[:, 1], s_load.at[6]),
        local(psi.at[:, 3 * c], pout, s_load.at[7]),
    ]
    for copy in loads:
        copy.start()
    row8 = lax.broadcasted_iota(jnp.int32, mo.shape, 0)
    mo[...] = jnp.where(row8 == 0, kept[0], jnp.where(row8 == 1, op[0], op[1]))
    mall[c] = mo[...]

    barrier = pltpu.get_barrier_semaphore()
    source = jnp.where(c == 0, up, down)
    greet = [partner, (source, 2 * x), (source, 2 * x + 1)]
    greet += [(s, 2 * t + h) for t in toward for h in range(2)]
    for dev in greet:
        pl.semaphore_signal(barrier, inc=1, device_id=dev, device_id_type=pl.DeviceIdType.MESH)
    pl.semaphore_wait(barrier, len(greet))

    give_left = [
        remote(left.at[:, chips[i]], lraw.at[own2, pl.ds(i * rc, rc)], s_pl.at[i], r_pl.at[i], partner)
        for i in range(4)
    ]
    give_right = remote(right, rown.at[own2], s_pr.at[0], r_pr.at[0], partner)
    give_meta = remote(mo, mall.at[c], s_pm.at[0], r_pm.at[0], partner)
    zdev = [(down, 2 * x), (up, 2 * x + 1)]
    half = size // 2
    give_z = [
        remote(
            right.at[:, pl.ds(h * half, half)], rnbr.at[own2, pl.ds(h * half, half)], s_zr.at[i, h], r_zr.at[c, h], zdev[i]
        )
        for h in range(2) for i in range(2)
    ]
    give_zm = [remote(mo, mz.at[c], s_zm.at[i], r_zm.at[c], zdev[i]) for i in range(2)]
    for copy in [give_meta, *give_left, give_right, *give_zm, *give_z]:
        copy.start()

    sign = jnp.where(c == 0, 0.5, -0.5).astype(F32)

    def scale_left(cc):
        for t in range(2):
            which = mall[cc, pl.ds(1 + t, 1), :]
            diag = jnp.where(which == 0, 1.0, jnp.where(which == 1, -0.25, 0.0))
            diag = jnp.where(which == 3, sign, jnp.where(which == 4, -sign, diag))
            flip = jnp.where(which == 2, 0.5, 0.0)
            outer = jnp.where(which == 0, 1.0, jnp.where(which == 1, 0.25, 0.0))
            outer = jnp.where(which >= 3, sign, outer)
            mat = lraw[2 * cc + t].astype(F32)
            lin[2 * cc + t, :, :size] = (mat * diag).astype(BF16)
            lin[2 * cc + t, :, size:] = (mat * flip).astype(BF16)
            lout[2 * cc + t] = (mat * outer).astype(BF16)

    for copy in loads[:5]:
        copy.wait()
    scale_left(c)
    give_meta.wait_recv()
    for copy in give_left:
        copy.wait_recv()
    scale_left(1 - c)
    give_right.wait_recv()
    for copy in loads[5:]:
        copy.wait()

    fb, nb, kf, rs, ry = (fb0, fb1), (nb0, nb1), (kf0, kf1), (rs0, rs1), (ry0, ry1)
    rx, po, loc = (rx0, rx1), (po0, po1), (loc0, loc1)

    def give_far(g, a, sgn):
        return remote(fb[g].at[a, sgn], ry[g].at[a, sgn], s_d2.at[g, a, sgn], r_ry.at[g, a, sgn], (s, 2 * toward[sgn] + c))

    def give_near(g, a, sgn, h):
        return remote(
            nb[g].at[a, sgn, h], rx[g].at[1 - sgn, c, a, sgn], s_dir.at[g, a, sgn, h], r_rx.at[g, 1 - sgn, c, a, sgn],
            (s, 2 * toward[1 - sgn] + h),
        )

    def give_relay(g, a, sgn, h):
        return remote(
            rs[g].at[a, sgn, h], rx[g].at[sgn, c, a, sgn], s_rel.at[g, a, sgn, h], r_rx.at[g, sgn, c, a, sgn],
            (s, 2 * toward[sgn] + h),
        )

    def give_chip(g, a, sgn):
        return remote(po[g].at[a, sgn], loc[g].at[c, a, sgn], s_po.at[g, a, sgn], r_po.at[g, a, sgn], partner)

    def parts_of(total):
        return [total[i * rc : (i + 1) * rc].reshape(2, rd, -1) for i in range(4)]

    def inner(jj, carry):
        for sgn in range(2):
            v = jj + 2 * sgn
            vec = pin[v].reshape(-1, size)
            total = jnp.zeros((size, size), F32)
            for t in range(4):
                lifted = jnp.dot(lin[t], vec, preferred_element_type=F32).astype(BF16)
                total += nt_dot(lifted, rown[t])
            column = lax.broadcasted_iota(jnp.int32, total.shape, 1)
            parts = parts_of(jnp.where(column < mine, total, 0.0))
            fb0[jj, sgn] = parts[0].astype(BF16)
            give_far(0, jj, sgn).start()
            nb0[jj, sgn] = parts[2 - sgn].astype(BF16)
            for h in range(2):
                give_near(0, jj, sgn, h).start()
            kf0[jj, sgn] = parts[1 + sgn]
            loc0[c, jj, sgn] = jnp.where(c == 0, parts[3][0], parts[3][1])
            po0[jj, sgn] = jnp.where(c == 0, parts[3][1], parts[3][0])
            give_chip(0, jj, sgn).start()
        return carry

    def lift_outer(v, carry):
        for t in range(4):
            lf[v, t] = jnp.dot(lout[t], pout[v], preferred_element_type=F32).astype(BF16)
        return carry

    def outer(a, limit):
        for sgn in range(2):
            for jj in range(2):
                total = jnp.zeros((size, half), F32)
                for t in range(4):
                    total += nt_dot(lf[2 * sgn + jj, t], rnbr[t, pl.ds(a * half, half), :])
                column = lax.broadcasted_iota(jnp.int32, total.shape, 1) + a * half
                parts = parts_of(jnp.where(column < limit, total, 0.0))
                fb1[a, sgn, :, jj] = parts[0].astype(BF16)
                nb1[a, sgn, :, jj] = parts[2 - sgn].astype(BF16)
                kf1[a, sgn, :, jj] = parts[1 + sgn]
                loc1[c, a, sgn, jj] = jnp.where(c == 0, parts[3][0], parts[3][1])
                po1[a, sgn, jj] = jnp.where(c == 0, parts[3][1], parts[3][0])
            give_far(1, a, sgn).start()
            give_chip(1, a, sgn).start()

    def nears(a):
        for sgn in range(2):
            for h in range(2):
                give_near(1, a, sgn, h).start()

    def relay(g, a):
        for sgn in range(2):
            give_far(g, a, sgn).wait_recv()
            rs[g][a, sgn] = (kf[g][a, sgn] + ry[g][a, sgn].astype(F32)).astype(BF16)
            for h in range(2):
                give_relay(g, a, sgn, h).start()

    row = lax.broadcasted_iota(jnp.int32, (rd, size), 0) + k * rd
    mine = mo[pl.ds(0, 1), :]

    def arrival(g, side, cc, a, sgn):
        piece = rx[g].at[side, cc, a, sgn]
        return remote(piece, piece, s_po.at[g, a, sgn], r_rx.at[g, side, cc, a, sgn], partner)

    def gathered(g, cc, a, sgn):
        for side in range(2):
            arrival(g, side, cc, a, sgn).wait_recv()
        total = loc[g][cc, a, sgn]
        for side in range(2):
            total += rx[g][side, cc, a, sgn].astype(F32)
        return total

    def finish_inner(jj, carry):
        for sgn in range(2):
            v = jj + 2 * sgn
            give_chip(0, jj, sgn).wait_recv()
            for cc in range(2):
                out[v, 1 + cc] = jnp.where(row < mine, gathered(0, cc, jj, sgn), 0.0)
        return carry

    def finish_outer(a):
        for sgn in range(2):
            give_chip(1, a, sgn).wait_recv()
            for cc in range(2):
                total = gathered(1, cc, a, sgn)
                for jj in range(2):
                    v = 2 * sgn + jj
                    out[v, 3 * cc, :, pl.ds(a * half, half)] = jnp.where(row[:, :half] < mine[:, :half], total[jj], 0.0)

    def wait_z(h):
        for cc in range(2):
            remote(
                right.at[:, pl.ds(h * half, half)], rnbr.at[pl.ds(2 * cc, 2), pl.ds(h * half, half)],
                s_zr.at[0, h], r_zr.at[cc, h], partner,
            ).wait_recv()

    lax.fori_loop(0, nvec // 2, inner, 0)
    lax.fori_loop(0, nvec, lift_outer, 0)
    relay(0, 0)
    for cc in range(2):
        remote(mo, mz.at[cc], s_zm.at[0], r_zm.at[cc], partner).wait_recv()
    edge = jnp.where(c == 0, sectors - 1, 0)
    limit = jnp.where(s == edge, 0, mz[0, pl.ds(0, 1), :])[:, :half]
    wait_z(0)
    outer(0, limit)
    relay(0, 1)
    wait_z(1)
    outer(1, limit)
    relay(1, 0)
    nears(0)
    nears(1)
    relay(1, 1)
    lax.fori_loop(0, nvec // 2, finish_inner, 0)
    finish_outer(0)
    finish_outer(1)

    for copy in [give_meta, *give_left, give_right, *give_z, *give_zm]:
        copy.wait_send()

    def drain(a, carry):
        for sgn in range(2):
            for g in range(2):
                give_far(g, a, sgn).wait_send()
                for h in range(2):
                    give_near(g, a, sgn, h).wait_send()
                    give_relay(g, a, sgn, h).wait_send()
                give_chip(g, a, sgn).wait_send()
        return carry

    lax.fori_loop(0, nvec // 2, drain, 0)


def shards(psi, left, right, op, kept):
    nvec, _, phys, size, _ = psi.shape
    rc, rd = size // NX, size // NX // 2
    sectors = lax.axis_size("sector")
    dma = pltpu.SemaphoreType.DMA
    vmem = pltpu.VMEM
    scratch = [
        vmem((nvec, 2, size, size), BF16),
        vmem((nvec, size, size), BF16),
        vmem((4, size, size), BF16),
        vmem((4, size, 2 * size), BF16),
        vmem((4, size, size), BF16),
        vmem((4, size, size), BF16),
        vmem((4, size, size), BF16),
        vmem((nvec, 4, size, size), BF16),
        vmem((8, size), jnp.int32),
        vmem((2, 8, size), jnp.int32),
        vmem((2, 8, size), jnp.int32),
    ]
    for piece in ((rd, size), (2, rd, size // 2)):
        scratch += [
            vmem((2, 2, 2, *piece), BF16),
            vmem((2, 2, 2, *piece), BF16),
            vmem((2, 2, 2, *piece), F32),
            vmem((2, 2, 2, *piece), BF16),
            vmem((2, 2, 2, *piece), BF16),
            vmem((2, 2, 2, 2, *piece), BF16),
            vmem((2, 2, *piece), F32),
            vmem((2, 2, 2, *piece), F32),
        ]
    scratch += [
        dma((8,)),
        dma((4,)), dma((4,)), dma((1,)), dma((1,)), dma((1,)), dma((1,)),
        dma((2, 2)), dma((2, 2)), dma((2,)), dma((2,)),
        dma((2, 2, 2)), dma((2, 2, 2)), dma((2, 2, 2, 2)), dma((2, 2, 2, 2)), dma((2, 2, 2, 2, 2)),
        dma((2, 2, 2)), dma((2, 2, 2)),
    ]
    anyspace = pl.BlockSpec(memory_space=pl.ANY)
    smem = pl.BlockSpec(memory_space=pltpu.SMEM)
    result = pl.pallas_call(
        functools.partial(kernel, sectors),
        out_shape=pltpu.VMEM((nvec, phys, rd, size), F32),
        in_specs=[anyspace, anyspace, anyspace, smem, smem],
        out_specs=pl.BlockSpec(memory_space=pltpu.VMEM),
        scratch_shapes=scratch,
        compiler_params=pltpu.CompilerParams(collective_id=0, has_side_effects=True, vmem_limit_bytes=56 * 2**20),
    )(
        psi.reshape(nvec, phys, size, size),
        left.reshape(2, NX, rc, size),
        right.reshape(2, size, size),
        op,
        kept,
    )
    return result[:, None]


def solution(mesh):
    in_specs = (
        P(None, "sector", None, None, None),
        P("term", "sector", None, None),
        P("term", "sector", None, None),
        P("term"),
        P("sector"),
    )
    out_specs = P(None, "sector", None, "term", None)
    return jax.shard_map(shards, mesh=mesh, in_specs=in_specs, out_specs=out_specs, check_vma=False)
```

```python
import functools

import jax
import jax.numpy as jnp
from jax import lax
from jax.experimental import pallas as pl
from jax.experimental.pallas import tpu as pltpu
from jax.sharding import PartitionSpec as P

F32 = jnp.float32
BF16 = jnp.bfloat16
NX = 4


def local(src, dst, sem):
    return pltpu.make_async_copy(src, dst, sem)


def remote(src, dst, send, recv, dev):
    return pltpu.make_async_remote_copy(
        src_ref=src, dst_ref=dst, send_sem=send, recv_sem=recv, device_id=dev, device_id_type=pl.DeviceIdType.MESH
    )


def nt_dot(a, b):
    return lax.dot_general(a, b, (((1,), (1,)), ((), ())), preferred_element_type=F32)


def kernel(
    sectors, psi, left, right, op, kept, out,
    pin, pout, lraw, lin, lout, rown, rnbr, lf, mo, mall, mz,
    fb0, nb0, kf0, rs0, ry0, rx0, po0, loc0, fb1, nb1, kf1, rs1, ry1, rx1, po1, loc1,
    s_load, s_pl, r_pl, s_pr, r_pr, s_pm, r_pm, s_zr, r_zr, s_zm, r_zm,
    s_d2, r_ry, s_dir, s_rel, r_rx, s_po, r_po,
):
    nvec, _, size, _ = psi.shape
    rc, rd = size // NX, size // NX // 2
    s = lax.axis_index("sector")
    k = lax.axis_index("term")
    x, c = lax.div(k, 2), lax.rem(k, 2)
    up = lax.rem(s + 1, sectors)
    down = lax.rem(s + sectors - 1, sectors)
    plus = lax.rem(x + 1, NX)
    minus = lax.rem(x + NX - 1, NX)
    partner = (s, 2 * x + 1 - c)
    own2 = pl.ds(2 * c, 2)
    chips = [lax.rem(x + off, NX) for off in (2, 1, 3, 0)]
    toward = [plus, minus]

    loads = [local(left.at[:, chips[i]], lraw.at[own2, pl.ds(i * rc, rc)], s_load.at[i]) for i in range(4)]
    loads += [
        local(right, rown.at[own2], s_load.at[4]),
        local(psi.at[:, 1 + c], pin.at[:, 0], s_load.at[5]),
        local(psi.at[:, 2 - c], pin.at[:, 1], s_load.at[6]),
        local(psi.at[:, 3 * c], pout, s_load.at[7]),
    ]
    for copy in loads:
        copy.start()
    row8 = lax.broadcasted_iota(jnp.int32, mo.shape, 0)
    mo[...] = jnp.where(row8 == 0, kept[0], jnp.where(row8 == 1, op[0], op[1]))
    mall[c] = mo[...]

    barrier = pltpu.get_barrier_semaphore()
    source = jnp.where(c == 0, up, down)
    greet = [partner, (source, 2 * x), (source, 2 * x + 1)]
    greet += [(s, 2 * t + h) for t in toward for h in range(2)]
    for dev in greet:
        pl.semaphore_signal(barrier, inc=1, device_id=dev, device_id_type=pl.DeviceIdType.MESH)
    pl.semaphore_wait(barrier, len(greet))

    give_left = [
        remote(left.at[:, chips[i]], lraw.at[own2, pl.ds(i * rc, rc)], s_pl.at[i], r_pl.at[i], partner)
        for i in range(4)
    ]
    give_right = remote(right, rown.at[own2], s_pr.at[0], r_pr.at[0], partner)
    give_meta = remote(mo, mall.at[c], s_pm.at[0], r_pm.at[0], partner)
    zdev = [(down, 2 * x), (up, 2 * x + 1)]
    half = size // 2
    give_z = [
        remote(
            right.at[:, pl.ds(h * half, half)], rnbr.at[own2, pl.ds(h * half, half)], s_zr.at[i, h], r_zr.at[c, h], zdev[i]
        )
        for h in range(2) for i in range(2)
    ]
    give_zm = [remote(mo, mz.at[c], s_zm.at[i], r_zm.at[c], zdev[i]) for i in range(2)]
    for copy in [give_meta, *give_left, give_right, *give_zm, *give_z]:
        copy.start()

    sign = jnp.where(c == 0, 0.5, -0.5).astype(F32)

    def scale_left(cc):
        for t in range(2):
            which = mall[cc, pl.ds(1 + t, 1), :]
            diag = jnp.where(which == 0, 1.0, jnp.where(which == 1, -0.25, 0.0))
            diag = jnp.where(which == 3, sign, jnp.where(which == 4, -sign, diag))
            flip = jnp.where(which == 2, 0.5, 0.0)
            outer = jnp.where(which == 0, 1.0, jnp.where(which == 1, 0.25, 0.0))
            outer = jnp.where(which >= 3, sign, outer)
            mat = lraw[2 * cc + t].astype(F32)
            lin[2 * cc + t, :, :size] = (mat * diag).astype(BF16)
            lin[2 * cc + t, :, size:] = (mat * flip).astype(BF16)
            lout[2 * cc + t] = (mat * outer).astype(BF16)

    for copy in loads[:5]:
        copy.wait()
    scale_left(c)
    give_meta.wait_recv()
    for copy in give_left:
        copy.wait_recv()
    scale_left(1 - c)
    give_right.wait_recv()
    for copy in loads[5:]:
        copy.wait()

    fb, nb, kf, rs, ry = (fb0, fb1), (nb0, nb1), (kf0, kf1), (rs0, rs1), (ry0, ry1)
    rx, po, loc = (rx0, rx1), (po0, po1), (loc0, loc1)

    def give_far(g, a, sgn):
        return remote(fb[g].at[a, sgn], ry[g].at[a, sgn], s_d2.at[g, a, sgn], r_ry.at[g, a, sgn], (s, 2 * toward[sgn] + c))

    def give_near(g, a, sgn, h):
        return remote(
            nb[g].at[a, sgn, h], rx[g].at[1 - sgn, c, a, sgn], s_dir.at[g, a, sgn, h], r_rx.at[g, 1 - sgn, c, a, sgn],
            (s, 2 * toward[1 - sgn] + h),
        )

    def give_relay(g, a, sgn, h):
        return remote(
            rs[g].at[a, sgn, h], rx[g].at[sgn, c, a, sgn], s_rel.at[g, a, sgn, h], r_rx.at[g, sgn, c, a, sgn],
            (s, 2 * toward[sgn] + h),
        )

    def give_chip(g, a, sgn):
        return remote(po[g].at[a, sgn], loc[g].at[c, a, sgn], s_po.at[g, a, sgn], r_po.at[g, a, sgn], partner)

    def parts_of(total):
        return [total[i * rc : (i + 1) * rc].reshape(2, rd, -1) for i in range(4)]

    def inner(jj, carry):
        for sgn in range(2):
            v = jj + 2 * sgn
            vec = pin[v].reshape(-1, size)
            total = jnp.zeros((size, size), F32)
            for t in range(4):
                lifted = jnp.dot(lin[t], vec, preferred_element_type=F32).astype(BF16)
                total += nt_dot(lifted, rown[t])
            column = lax.broadcasted_iota(jnp.int32, total.shape, 1)
            parts = parts_of(jnp.where(column < mine, total, 0.0))
            fb0[jj, sgn] = parts[0].astype(BF16)
            give_far(0, jj, sgn).start()
            nb0[jj, sgn] = parts[2 - sgn].astype(BF16)
            for h in range(2):
                give_near(0, jj, sgn, h).start()
            kf0[jj, sgn] = parts[1 + sgn]
            loc0[c, jj, sgn] = jnp.where(c == 0, parts[3][0], parts[3][1])
            po0[jj, sgn] = jnp.where(c == 0, parts[3][1], parts[3][0])
            give_chip(0, jj, sgn).start()
        return carry

    def lift_outer(v, carry):
        for t in range(4):
            lf[v, t] = jnp.dot(lout[t], pout[v], preferred_element_type=F32).astype(BF16)
        return carry

    def outer(a, limit):
        for sgn in range(2):
            for jj in range(2):
                total = jnp.zeros((size, half), F32)
                for t in range(4):
                    total += nt_dot(lf[2 * sgn + jj, t], rnbr[t, pl.ds(a * half, half), :])
                column = lax.broadcasted_iota(jnp.int32, total.shape, 1) + a * half
                parts = parts_of(jnp.where(column < limit, total, 0.0))
                fb1[a, sgn, :, jj] = parts[0].astype(BF16)
                nb1[a, sgn, :, jj] = parts[2 - sgn].astype(BF16)
                kf1[a, sgn, :, jj] = parts[1 + sgn]
                loc1[c, a, sgn, jj] = jnp.where(c == 0, parts[3][0], parts[3][1])
                po1[a, sgn, jj] = jnp.where(c == 0, parts[3][1], parts[3][0])
            give_far(1, a, sgn).start()
            give_chip(1, a, sgn).start()

    def nears(a):
        for sgn in range(2):
            for h in range(2):
                give_near(1, a, sgn, h).start()

    def relay(g, a):
        for sgn in range(2):
            give_far(g, a, sgn).wait_recv()
            rs[g][a, sgn] = (kf[g][a, sgn] + ry[g][a, sgn].astype(F32)).astype(BF16)
            for h in range(2):
                give_relay(g, a, sgn, h).start()

    row = lax.broadcasted_iota(jnp.int32, (rd, size), 0) + k * rd
    mine = mo[pl.ds(0, 1), :]

    def arrival(g, side, cc, a, sgn):
        piece = rx[g].at[side, cc, a, sgn]
        return remote(piece, piece, s_po.at[g, a, sgn], r_rx.at[g, side, cc, a, sgn], partner)

    def gathered(g, cc, a, sgn):
        for side in range(2):
            arrival(g, side, cc, a, sgn).wait_recv()
        total = loc[g][cc, a, sgn]
        for side in range(2):
            total += rx[g][side, cc, a, sgn].astype(F32)
        return total

    def finish_inner(jj, carry):
        for sgn in range(2):
            v = jj + 2 * sgn
            give_chip(0, jj, sgn).wait_recv()
            for cc in range(2):
                out[v, 1 + cc] = jnp.where(row < mine, gathered(0, cc, jj, sgn), 0.0)
        return carry

    def finish_outer(a):
        for sgn in range(2):
            give_chip(1, a, sgn).wait_recv()
            for cc in range(2):
                total = gathered(1, cc, a, sgn)
                for jj in range(2):
                    v = 2 * sgn + jj
                    out[v, 3 * cc, :, pl.ds(a * half, half)] = jnp.where(row[:, :half] < mine[:, :half], total[jj], 0.0)

    def wait_z(h):
        for cc in range(2):
            remote(
                right.at[:, pl.ds(h * half, half)], rnbr.at[pl.ds(2 * cc, 2), pl.ds(h * half, half)],
                s_zr.at[0, h], r_zr.at[cc, h], partner,
            ).wait_recv()

    lax.fori_loop(0, nvec // 2, inner, 0)
    lax.fori_loop(0, nvec, lift_outer, 0)
    relay(0, 0)
    for cc in range(2):
        remote(mo, mz.at[cc], s_zm.at[0], r_zm.at[cc], partner).wait_recv()
    edge = jnp.where(c == 0, sectors - 1, 0)
    limit = jnp.where(s == edge, 0, mz[0, pl.ds(0, 1), :])[:, :half]
    relay(0, 1)
    wait_z(0)
    outer(0, limit)
    wait_z(1)
    outer(1, limit)
    relay(1, 0)
    nears(0)
    nears(1)
    relay(1, 1)
    lax.fori_loop(0, nvec // 2, finish_inner, 0)
    finish_outer(0)
    finish_outer(1)

    for copy in [give_meta, *give_left, give_right, *give_z, *give_zm]:
        copy.wait_send()

    def drain(a, carry):
        for sgn in range(2):
            for g in range(2):
                give_far(g, a, sgn).wait_send()
                for h in range(2):
                    give_near(g, a, sgn, h).wait_send()
                    give_relay(g, a, sgn, h).wait_send()
                give_chip(g, a, sgn).wait_send()
        return carry

    lax.fori_loop(0, nvec // 2, drain, 0)


def shards(psi, left, right, op, kept):
    nvec, _, phys, size, _ = psi.shape
    rc, rd = size // NX, size // NX // 2
    sectors = lax.axis_size("sector")
    dma = pltpu.SemaphoreType.DMA
    vmem = pltpu.VMEM
    scratch = [
        vmem((nvec, 2, size, size), BF16),
        vmem((nvec, size, size), BF16),
        vmem((4, size, size), BF16),
        vmem((4, size, 2 * size), BF16),
        vmem((4, size, size), BF16),
        vmem((4, size, size), BF16),
        vmem((4, size, size), BF16),
        vmem((nvec, 4, size, size), BF16),
        vmem((8, size), jnp.int32),
        vmem((2, 8, size), jnp.int32),
        vmem((2, 8, size), jnp.int32),
    ]
    for piece in ((rd, size), (2, rd, size // 2)):
        scratch += [
            vmem((2, 2, 2, *piece), BF16),
            vmem((2, 2, 2, *piece), BF16),
            vmem((2, 2, 2, *piece), F32),
            vmem((2, 2, 2, *piece), BF16),
            vmem((2, 2, 2, *piece), BF16),
            vmem((2, 2, 2, 2, *piece), BF16),
            vmem((2, 2, *piece), F32),
            vmem((2, 2, 2, *piece), F32),
        ]
    scratch += [
        dma((8,)),
        dma((4,)), dma((4,)), dma((1,)), dma((1,)), dma((1,)), dma((1,)),
        dma((2, 2)), dma((2, 2)), dma((2,)), dma((2,)),
        dma((2, 2, 2)), dma((2, 2, 2)), dma((2, 2, 2, 2)), dma((2, 2, 2, 2)), dma((2, 2, 2, 2, 2)),
        dma((2, 2, 2)), dma((2, 2, 2)),
    ]
    anyspace = pl.BlockSpec(memory_space=pl.ANY)
    smem = pl.BlockSpec(memory_space=pltpu.SMEM)
    result = pl.pallas_call(
        functools.partial(kernel, sectors),
        out_shape=pltpu.VMEM((nvec, phys, rd, size), F32),
        in_specs=[anyspace, anyspace, anyspace, smem, smem],
        out_specs=pl.BlockSpec(memory_space=pltpu.VMEM),
        scratch_shapes=scratch,
        compiler_params=pltpu.CompilerParams(collective_id=0, has_side_effects=True, vmem_limit_bytes=56 * 2**20),
    )(
        psi.reshape(nvec, phys, size, size),
        left.reshape(2, NX, rc, size),
        right.reshape(2, size, size),
        op,
        kept,
    )
    return result[:, None]


def solution(mesh):
    in_specs = (
        P(None, "sector", None, None, None),
        P("term", "sector", None, None),
        P("term", "sector", None, None),
        P("term"),
        P("sector"),
    )
    out_specs = P(None, "sector", None, "term", None)
    return jax.shard_map(shards, mesh=mesh, in_specs=in_specs, out_specs=out_specs, check_vma=False)
```
